32 devices in a mesh: section: 8 (over y, x, core), fsdp: 4 (over z).
Axes of the slice: x: 2, y: 2, z: 4, core: 2. Of those that a mesh axis runs over, the one named last changes fastest.
Arguments:
- layer_input: bfloat16 [8, 512, 4096], P('section', 'fsdp'), may hold values from -6 to 6
- next_cot: bfloat16 [8, 512, 512], P('section', 'fsdp'), may hold values from -6 to 6
- w_value: bfloat16 [8, 4096, 512], P('section', 'fsdp'), may hold values from -0.25 to 0.25
- micro_ids: int32 [8, 4], P('section', 'fsdp'), may hold values from 0 to 1
Outputs:
- grad_input: bfloat16 [8, 512, 4096], P('section', 'fsdp')
- grad_sum: float32 [8, 4096, 512], P('section', 'fsdp')
- grad_square: float32 [8, 4096, 512], P('section', 'fsdp')
The draws below stay inside these ranges and needn't reach their ends.
All inputs are finite; a program needn't handle non-finite values.
Results may differ from the reference program's by a relative error of at most 0.0037.
Values may be sent and summed in bfloat16 or wider, within the bound.
A program may use at most 64 MiB of HBM per device.

```python
import jax
import jax.numpy as jnp
from jax import lax

D = 4096
MICRO = 2
TOK_DEV = 128
KVC = 512
TOKF = 512
N_SECTION = 8
N_FSDP = 4


def plant(drawn, rng, low, top_value):
    extent = drawn.shape
    place = [jax.random.randint(jax.random.fold_in(rng, axis), (), 0, extent[axis]) for axis in range(len(extent))]
    drawn = drawn.at[tuple(place)].set(low)
    longest = extent.index(max(extent))
    place[longest] = (place[longest] + 1) % extent[longest]
    return drawn.at[tuple(place)].set(top_value)


def raised(values, own_key, source, target, parts, factor):
    owner, partner = [(jnp.arange(values.shape[position]) // (values.shape[position] // parts)).reshape([-1 if axis == position else 1 for axis in range(values.ndim)]) for position in (source, target)]
    chosen = jax.random.permutation(own_key, parts)[partner]
    strong = (owner == chosen) | (owner == (partner + parts // 2) % parts)
    return jnp.where(strong, factor * values, values)


def steps_of(key, extent, cuts, smallest, top_value):
    gain, own = 1.0, jax.random.fold_in(key, 6)
    for position, blocks in cuts:
        heights = jnp.exp(jax.random.uniform(jax.random.fold_in(own, position), (blocks,), jnp.float32, smallest / len(cuts), top_value / len(cuts)))
        gain = gain * jnp.repeat(heights, extent[position] // blocks).reshape([-1 if axis == position else 1 for axis in range(len(extent))])
    return gain


def bell_draw(stream_key, extent, scale, most, shards=(), kind=jnp.bfloat16):
    level = steps_of(stream_key, extent, shards, -0.22, 0.18) if shards else 1.0
    entries = jax.random.normal(stream_key, extent, jnp.float32) * scale * level
    return jnp.minimum(jnp.maximum(entries, -most), most).astype(kind)


def bell_draw_with(key, extent, scale, most, cuts, heavy, kind=jnp.bfloat16):
    entries = scale * jax.random.normal(key, extent, jnp.float32)
    if cuts:
        entries = entries * steps_of(key, extent, cuts, -0.22, 0.18)
    return jnp.clip(raised(entries, jax.random.fold_in(key, 3), *heavy), -most, most).astype(kind)


def setup_inputs(seed: int = 0) -> dict:
    arg_keys = jax.random.split(jax.random.key(seed), 5)
    return {
        "layer_input": bell_draw_with(arg_keys[0], (N_SECTION, TOKF, D), 1.0, 6.0, ((0, 8), (1, 4)), (1, 2, 4, 2.0)),
        "next_cot": bell_draw(arg_keys[1], (N_SECTION, TOKF, KVC), 1.0, 6.0, ((0, 8), (1, 4))),
        "w_value": bell_draw(arg_keys[2], (N_SECTION, D, KVC), KVC ** -0.5, 0.25, ((0, 8), (1, 4))),
        "micro_ids": plant(jax.random.randint(arg_keys[3], (N_SECTION, N_FSDP), 0, MICRO), jax.random.fold_in(arg_keys[3], 1), 0, MICRO - 1).astype(jnp.int32),
    }


def one_section(operands):
    inputs_section, cot_section, weight_section, micro_section = operands
    grad_in = jnp.dot(cot_section, weight_section.T, preferred_element_type=jnp.float32).astype(jnp.bfloat16)
    blocks_in = inputs_section.reshape(N_FSDP, TOK_DEV, D).astype(jnp.float32)
    blocks_cot = cot_section.reshape(N_FSDP, TOK_DEV, KVC).astype(jnp.float32)
    partial_value = jnp.einsum('ftd,ftc->fdc', blocks_in, blocks_cot) * (1.0 / TOK_DEV)
    partial_value = lax.optimization_barrier(partial_value.astype(jnp.bfloat16)).astype(jnp.float32)
    onehot = (micro_section[:, None] == jnp.arange(MICRO, dtype=jnp.int32)[None, :]).astype(jnp.float32)
    per_micro = jnp.einsum('fm,fdc->mdc', onehot, partial_value)
    return grad_in, jnp.sum(per_micro, axis=0), jnp.sum(per_micro * per_micro, axis=0)


def reference(layer_input, next_cot, w_value, micro_ids):
    incoming = jnp.roll(next_cot, -1, axis=0)
    grad_input, grad_sum, grad_square = lax.map(one_section, (layer_input, incoming, w_value, micro_ids))
    return (grad_input, grad_sum, grad_square)
```

```python
import functools

import jax
import jax.numpy as jnp
from jax import lax
from jax.experimental import pallas as pl
from jax.experimental.pallas import tpu as pltpu
from jax.sharding import PartitionSpec as P

MICRO = 2
MESH = pl.DeviceIdType.MESH


def kernel(
    n, ns, li, cot, w, mid, gi, gs, gq,
    inc, lix, gis, ids, wv,
    perm_s, perm_r, right_s, left_s, cot_r, li_s, li_r, gi_s, gi_r, id_s, id_r, own_s,
):
    f = lax.axis_index("fsdp")
    s = lax.axis_index("section")
    behind = lax.rem(s + ns - 1, ns)
    ahead = lax.rem(s + 1, ns)
    tokens, share = lix.shape[1], lix.shape[2]
    columns = inc.shape[2]

    def share_of(ref, part, rows=slice(None)):
        return ref.at[rows, pl.ds(pl.multiple_of(part * share, share), share)]

    def li_copy(target, rows=slice(None)):
        return pltpu.make_async_remote_copy(
            src_ref=share_of(li, target, rows),
            dst_ref=lix.at[f, rows],
            send_sem=li_s.at[target],
            recv_sem=li_r.at[f],
            device_id={"fsdp": target},
            device_id_type=MESH,
        )

    def cot_copy(block, target, sem):
        return pltpu.make_async_remote_copy(
            src_ref=inc.at[block],
            dst_ref=inc.at[block],
            send_sem=sem.at[block],
            recv_sem=cot_r.at[block],
            device_id={"fsdp": target},
            device_id_type=MESH,
        )

    def gi_copy(target):
        return pltpu.make_async_remote_copy(
            src_ref=gis.at[target],
            dst_ref=share_of(gi, f),
            send_sem=gi_s.at[target],
            recv_sem=gi_r.at[f],
            device_id={"fsdp": target},
            device_id_type=MESH,
        )

    def id_copy(target):
        return pltpu.make_async_remote_copy(
            src_ref=ids.at[f],
            dst_ref=ids.at[f],
            send_sem=id_s.at[target],
            recv_sem=id_r.at[f],
            device_id={"fsdp": target},
            device_id_type=MESH,
        )

    weights = pltpu.make_async_copy(w, wv, own_s.at[0])
    weights.start()
    own_li = pltpu.make_async_copy(share_of(li, f), lix.at[f], own_s.at[1])
    own_li.start()
    ids[f] = jnp.full(ids.shape[1:], mid[0, 0], jnp.int32)

    barrier = pltpu.get_barrier_semaphore()
    for peer in (behind, ahead):
        pl.semaphore_signal(barrier, inc=1, device_id={"section": peer}, device_id_type=MESH)
    for step in range(1, n):
        pl.semaphore_signal(
            barrier, inc=1, device_id={"fsdp": lax.rem(f + step, n)}, device_id_type=MESH
        )
    pl.semaphore_wait(barrier, n + 1)

    permute = pltpu.make_async_remote_copy(
        src_ref=cot,
        dst_ref=inc.at[f],
        send_sem=perm_s,
        recv_sem=perm_r,
        device_id={"section": behind},
        device_id_type=MESH,
    )
    permute.start()

    pieces = min(n, 4)
    rows = tokens // pieces

    def li_piece(piece):
        if piece >= pieces:
            return
        window = pl.ds(piece * rows, rows)

        @pl.when(f < n - 1)
        def _():
            li_copy(n - 1, window).start()

        @pl.when(f > 0)
        def _():
            li_copy(0, window).start()

    def forward(step):
        @pl.when((f - step >= 0) & (f < n - 1))
        def _():
            cot_copy(f - step, f + 1, right_s).start()

        @pl.when((f + step < n) & (f > 0))
        def _():
            cot_copy(f + step, f - 1, left_s).start()

    def arrived(step):
        @pl.when(f - step >= 0)
        def _():
            cot_copy(f - step, f, right_s).wait_recv()

        @pl.when(f + step < n)
        def _():
            cot_copy(f + step, f, left_s).wait_recv()

    li_piece(0)
    permute.wait_recv()
    forward(0)
    for step in range(1, n):
        id_copy(lax.rem(f + step, n)).start()
    li_piece(1)
    for step in range(1, n - 1):
        arrived(step)
        forward(step)
        li_piece(step + 1)
    for piece in range(n, pieces):
        li_piece(piece)
    for turn in range(1, n - 1):
        @pl.when(n - 1 - turn > f)
        def _():
            li_copy(n - 1 - turn).start()

        @pl.when(turn < f)
        def _():
            li_copy(turn).start()
    arrived(n - 1)

    weights.wait()

    def input_block(block, carry):
        gis[block] = lax.dot_general(
            inc[block], wv[...], (((1,), (1,)), ((), ())), preferred_element_type=jnp.float32
        ).astype(gis.dtype)
        return carry

    lax.fori_loop(0, n, input_block, 0)
    own_gi = pltpu.make_async_copy(gis.at[f], share_of(gi, f), own_s.at[2])
    own_gi.start()
    for turn in range(n - 1):
        @pl.when(n - 1 - turn > f)
        def _():
            gi_copy(n - 1 - turn).start()

        @pl.when(turn < f)
        def _():
            gi_copy(turn).start()

    own_li.wait()

    def others(action):
        def run(step, carry):
            action(lax.rem(f + step, n))
            return carry

        lax.fori_loop(1, n, run, 0)

    def li_wait(peer):
        pltpu.make_async_remote_copy(
            src_ref=share_of(li, peer),
            dst_ref=lix.at[peer],
            send_sem=li_s.at[peer],
            recv_sem=li_r.at[peer],
            device_id={"fsdp": peer},
            device_id_type=MESH,
        ).wait()
        pltpu.make_async_remote_copy(
            src_ref=ids.at[f],
            dst_ref=ids.at[peer],
            send_sem=id_s.at[peer],
            recv_sem=id_r.at[peer],
            device_id={"fsdp": peer},
            device_id_type=MESH,
        ).wait()

    others(li_wait)

    inverse = 1.0 / tokens
    tile = 128

    def weight_rows(index, carry):
        start = pl.multiple_of(index * tile, tile)
        micro = [jnp.zeros((tile, columns), jnp.float32) for _ in range(MICRO)]
        for block in range(n):
            product = lax.dot_general(
                lix[block, :, pl.ds(start, tile)],
                inc[block],
                (((0,), (0,)), ((), ())),
                preferred_element_type=jnp.float32,
            )
            product = (product * inverse).astype(jnp.bfloat16).astype(jnp.float32)
            owner = jnp.broadcast_to(ids[block][:1, :1], product.shape)
            for m in range(MICRO):
                micro[m] = micro[m] + jnp.where(owner == m, product, 0.0)
        total = micro[0]
        square = micro[0] * micro[0]
        for m in range(1, MICRO):
            total = total + micro[m]
            square = square + micro[m] * micro[m]
        gs[pl.ds(start, tile), :] = total
        gq[pl.ds(start, tile), :] = square
        return carry

    lax.fori_loop(0, share // tile, weight_rows, 0)

    own_gi.wait()
    permute.wait_send()
    for step in range(n - 1):
        @pl.when((f - step >= 0) & (f < n - 1))
        def _():
            cot_copy(f - step, f + 1, right_s).wait_send()

        @pl.when((f + step < n) & (f > 0))
        def _():
            cot_copy(f + step, f - 1, left_s).wait_send()

    def gi_wait(peer):
        pltpu.make_async_remote_copy(
            src_ref=gis.at[peer],
            dst_ref=share_of(gi, peer),
            send_sem=gi_s.at[peer],
            recv_sem=gi_r.at[peer],
            device_id={"fsdp": peer},
            device_id_type=MESH,
        ).wait()

    others(gi_wait)


def body(layer_input, next_cot, w_value, micro_ids):
    n = lax.axis_size("fsdp")
    ns = lax.axis_size("section")
    tokens, width = layer_input.shape[1:]
    share, columns = w_value.shape[1:]
    anywhere = pl.BlockSpec(memory_space=pltpu.HBM)
    dma = pltpu.SemaphoreType.DMA
    grad_input, grad_sum, grad_square = pl.pallas_call(
        functools.partial(kernel, n, ns),
        out_shape=(
            jax.ShapeDtypeStruct((tokens, width), jnp.bfloat16),
            jax.ShapeDtypeStruct((share, columns), jnp.float32),
            jax.ShapeDtypeStruct((share, columns), jnp.float32),
        ),
        in_specs=[anywhere, anywhere, anywhere, pl.BlockSpec(memory_space=pltpu.SMEM)],
        out_specs=OUT_SPECS,
        scratch_shapes=[
            pltpu.VMEM((n, tokens, columns), jnp.bfloat16),
            pltpu.VMEM((n, tokens, share), jnp.bfloat16),
            pltpu.VMEM((n, tokens, share), jnp.bfloat16),
            pltpu.VMEM((n, 8, 128), jnp.int32),
            pltpu.VMEM((share, columns), jnp.bfloat16),
            dma, dma, dma((n,)), dma((n,)), dma((n,)), dma((n,)), dma((n,)),
            dma((n,)), dma((n,)), dma((n,)), dma((n,)), dma((3,)),
        ],
        compiler_params=pltpu.CompilerParams(
            collective_id=0, has_side_effects=True, vmem_limit_bytes=40 * 2**20
        ),
    )(layer_input[0], next_cot[0], w_value[0], micro_ids)
    return (grad_input[None], grad_sum[None], grad_square[None])


OUT_SPECS = (
    pl.BlockSpec(memory_space=pl.ANY),
    pl.BlockSpec(memory_space=pltpu.VMEM),
    pl.BlockSpec(memory_space=pltpu.VMEM),
)


def solution(mesh):
    spec = P("section", "fsdp", None)
    return jax.shard_map(
        body,
        mesh=mesh,
        in_specs=(spec, spec, spec, P("section", "fsdp")),
        out_specs=(spec, spec, spec),
        check_vma=False,
    )
```

```python
import functools

import jax
import jax.numpy as jnp
from jax import lax
from jax.experimental import pallas as pl
from jax.experimental.pallas import tpu as pltpu
from jax.sharding import PartitionSpec as P

MICRO = 2
MESH = pl.DeviceIdType.MESH


def kernel(
    n, ns, li, cot, w, mid, gi, gs, gq,
    inc, lix, gis, ids, wv,
    perm_s, perm_r, right_s, left_s, cot_r, li_s, li_r, gi_s, gi_r, id_s, id_r, own_s,
):
    f = lax.axis_index("fsdp")
    s = lax.axis_index("section")
    behind = lax.rem(s + ns - 1, ns)
    ahead = lax.rem(s + 1, ns)
    tokens, share = lix.shape[1], lix.shape[2]
    columns = inc.shape[2]

    def share_of(ref, part, rows=slice(None)):
        return ref.at[rows, pl.ds(pl.multiple_of(part * share, share), share)]

    def li_copy(target, rows=slice(None)):
        return pltpu.make_async_remote_copy(
            src_ref=share_of(li, target, rows),
            dst_ref=lix.at[f, rows],
            send_sem=li_s.at[target],
            recv_sem=li_r.at[f],
            device_id={"fsdp": target},
            device_id_type=MESH,
        )

    def cot_copy(block, target, sem):
        return pltpu.make_async_remote_copy(
            src_ref=inc.at[block],
            dst_ref=inc.at[block],
            send_sem=sem.at[block],
            recv_sem=cot_r.at[block],
            device_id={"fsdp": target},
            device_id_type=MESH,
        )

    def gi_copy(target):
        return pltpu.make_async_remote_copy(
            src_ref=gis.at[target],
            dst_ref=share_of(gi, f),
            send_sem=gi_s.at[target],
            recv_sem=gi_r.at[f],
            device_id={"fsdp": target},
            device_id_type=MESH,
        )

    def id_copy(target):
        return pltpu.make_async_remote_copy(
            src_ref=ids.at[f],
            dst_ref=ids.at[f],
            send_sem=id_s.at[target],
            recv_sem=id_r.at[f],
            device_id={"fsdp": target},
            device_id_type=MESH,
        )

    weights = pltpu.make_async_copy(w, wv, own_s.at[0])
    weights.start()
    own_li = pltpu.make_async_copy(share_of(li, f), lix.at[f], own_s.at[1])
    own_li.start()
    ids[f] = jnp.full(ids.shape[1:], mid[0, 0], jnp.int32)

    barrier = pltpu.get_barrier_semaphore()
    for peer in (behind, ahead):
        pl.semaphore_signal(barrier, inc=1, device_id={"section": peer}, device_id_type=MESH)
    for step in range(1, n):
        pl.semaphore_signal(
            barrier, inc=1, device_id={"fsdp": lax.rem(f + step, n)}, device_id_type=MESH
        )
    pl.semaphore_wait(barrier, n + 1)

    permute = pltpu.make_async_remote_copy(
        src_ref=cot,
        dst_ref=inc.at[f],
        send_sem=perm_s,
        recv_sem=perm_r,
        device_id={"section": behind},
        device_id_type=MESH,
    )
    permute.start()

    pieces = min(n, 4)
    rows = tokens // pieces

    def li_piece(piece):
        if piece >= pieces:
            return
        window = pl.ds(piece * rows, rows)

        @pl.when(f < n - 1)
        def _():
            li_copy(n - 1, window).start()

        @pl.when(f > 0)
        def _():
            li_copy(0, window).start()

    def forward(step):
        @pl.when((f - step >= 0) & (f < n - 1))
        def _():
            cot_copy(f - step, f + 1, right_s).start()

        @pl.when((f + step < n) & (f > 0))
        def _():
            cot_copy(f + step, f - 1, left_s).start()

    def arrived(step):
        @pl.when(f - step >= 0)
        def _():
            cot_copy(f - step, f, right_s).wait_recv()

        @pl.when(f + step < n)
        def _():
            cot_copy(f + step, f, left_s).wait_recv()

    li_piece(0)
    permute.wait_recv()
    forward(0)
    for step in range(1, n):
        id_copy(lax.rem(f + step, n)).start()
    li_piece(1)
    for step in range(1, n - 1):
        arrived(step)
        forward(step)
        li_piece(step + 1)
    for piece in range(n, pieces):
        li_piece(piece)
    for turn in range(1, n - 1):
        @pl.when(n - 1 - turn > f)
        def _():
            li_copy(n - 1 - turn).start()

        @pl.when(turn < f)
        def _():
            li_copy(turn).start()
    arrived(n - 1)

    weights.wait()

    def input_block(block, carry):
        gis[block] = lax.dot_general(
            inc[block], wv[...], (((1,), (1,)), ((), ())), preferred_element_type=jnp.float32
        ).astype(gis.dtype)
        return carry

    lax.fori_loop(0, n, input_block, 0)
    own_gi = pltpu.make_async_copy(gis.at[f], share_of(gi, f), own_s.at[2])
    own_gi.start()
    for turn in range(n - 1):
        @pl.when(n - 1 - turn > f)
        def _():
            gi_copy(n - 1 - turn).start()

        @pl.when(turn < f)
        def _():
            gi_copy(turn).start()

    own_li.wait()

    def others(action):
        def run(step, carry):
            action(lax.rem(f + step, n))
            return carry

        lax.fori_loop(1, n, run, 0)

    def li_wait(peer):
        pltpu.make_async_remote_copy(
            src_ref=share_of(li, peer),
            dst_ref=lix.at[peer],
            send_sem=li_s.at[peer],
            recv_sem=li_r.at[peer],
            device_id={"fsdp": peer},
            device_id_type=MESH,
        ).wait()
        pltpu.make_async_remote_copy(
            src_ref=ids.at[f],
            dst_ref=ids.at[peer],
            send_sem=id_s.at[peer],
            recv_sem=id_r.at[peer],
            device_id={"fsdp": peer},
            device_id_type=MESH,
        ).wait()

    others(li_wait)

    inverse = 1.0 / tokens
    tile = 128

    def weight_rows(index, carry):
        start = pl.multiple_of(index * tile, tile)
        micro = [jnp.zeros((tile, columns), jnp.float32) for _ in range(MICRO)]
        for block in range(n):
            product = lax.dot_general(
                lix[block, :, pl.ds(start, tile)],
                inc[block],
                (((0,), (0,)), ((), ())),
                preferred_element_type=jnp.float32,
            )
            product = (product * inverse).astype(jnp.bfloat16).astype(jnp.float32)
            owner = jnp.broadcast_to(ids[block][:1, :1], product.shape)
            for m in range(MICRO):
                micro[m] = micro[m] + jnp.where(owner == m, product, 0.0)
        total = micro[0]
        square = micro[0] * micro[0]
        for m in range(1, MICRO):
            total = total + micro[m]
            square = square + micro[m] * micro[m]
        gs[pl.ds(start, tile), :] = total
        gq[pl.ds(start, tile), :] = square
        return carry

    lax.fori_loop(0, share // tile, weight_rows, 0)

    own_gi.wait()
    permute.wait_send()
    for step in range(n - 1):
        @pl.when((f - step >= 0) & (f < n - 1))
        def _():
            cot_copy(f - step, f + 1, right_s).wait_send()

        @pl.when((f + step < n) & (f > 0))
        def _():
            cot_copy(f + step, f - 1, left_s).wait_send()

    def gi_wait(peer):
        pltpu.make_async_remote_copy(
            src_ref=gis.at[peer],
            dst_ref=share_of(gi, peer),
            send_sem=gi_s.at[peer],
            recv_sem=gi_r.at[peer],
            device_id={"fsdp": peer},
            device_id_type=MESH,
        ).wait()

    others(gi_wait)


def settle_kernel(cuts, *refs):
    count = len(refs) // 2
    sems = refs[-1]
    copies = []
    for index in range(count):
        source, target = refs[index], refs[count + index]
        rows = source.shape[0] // cuts
        for cut in range(cuts):
            window = pl.ds(cut * rows, rows)
            copies.append(
                pltpu.make_async_copy(source.at[window], target.at[window], sems.at[index, cut])
            )
    for copy in copies:
        copy.start()
    for copy in copies:
        copy.wait()


def settle(*arrays):
    cuts = 1
    return pl.pallas_call(
        functools.partial(settle_kernel, cuts),
        out_shape=tuple(jax.ShapeDtypeStruct(a.shape, a.dtype) for a in arrays),
        in_specs=[pl.BlockSpec(memory_space=pl.ANY)] * len(arrays),
        out_specs=tuple(pl.BlockSpec(memory_space=pltpu.HBM) for _ in arrays),
        scratch_shapes=[pltpu.SemaphoreType.DMA((len(arrays), cuts))],
        compiler_params=pltpu.CompilerParams(vmem_limit_bytes=4 * 2**20),
    )(*[pltpu.with_memory_space_constraint(a, pltpu.VMEM) for a in arrays])


def body(layer_input, next_cot, w_value, micro_ids):
    n = lax.axis_size("fsdp")
    ns = lax.axis_size("section")
    tokens, width = layer_input.shape[1:]
    share, columns = w_value.shape[1:]
    anywhere = pl.BlockSpec(memory_space=pltpu.HBM)
    dma = pltpu.SemaphoreType.DMA
    stay = functools.partial(pltpu.with_memory_space_constraint, memory_space=pltpu.HBM)
    arrays = pl.pallas_call(
        functools.partial(kernel, n, ns),
        out_shape=(
            jax.ShapeDtypeStruct((tokens, width), jnp.bfloat16),
            jax.ShapeDtypeStruct((share, columns), jnp.float32),
            jax.ShapeDtypeStruct((share, columns), jnp.float32),
        ),
        in_specs=[anywhere, anywhere, anywhere, pl.BlockSpec(memory_space=pltpu.SMEM)],
        out_specs=OUT_SPECS,
        scratch_shapes=[
            pltpu.VMEM((n, tokens, columns), jnp.bfloat16),
            pltpu.VMEM((n, tokens, share), jnp.bfloat16),
            pltpu.VMEM((n, tokens, share), jnp.bfloat16),
            pltpu.VMEM((n, 8, 128), jnp.int32),
            pltpu.VMEM((share, columns), jnp.bfloat16),
            dma, dma, dma((n,)), dma((n,)), dma((n,)), dma((n,)), dma((n,)),
            dma((n,)), dma((n,)), dma((n,)), dma((n,)), dma((3,)),
        ],
        compiler_params=pltpu.CompilerParams(
            collective_id=0, has_side_effects=True, vmem_limit_bytes=40 * 2**20
        ),
    )(stay(layer_input[0]), stay(next_cot[0]), stay(w_value[0]), micro_ids)
    grad_input, grad_sum, grad_square = settle(*arrays)
    return (grad_input[None], grad_sum[None], grad_square[None])


OUT_SPECS = (
    pl.BlockSpec(memory_space=pl.ANY),
    pl.BlockSpec(memory_space=pltpu.VMEM),
    pl.BlockSpec(memory_space=pltpu.VMEM),
)


def solution(mesh):
    spec = P("section", "fsdp", None)
    return jax.shard_map(
        body,
        mesh=mesh,
        in_specs=(spec, spec, spec, P("section", "fsdp")),
        out_specs=(spec, spec, spec),
        check_vma=False,
    )
```

```python
import functools

import jax
import jax.numpy as jnp
from jax import lax
from jax.experimental import pallas as pl
from jax.experimental.pallas import tpu as pltpu
from jax.sharding import PartitionSpec as P

MICRO = 2
MESH = pl.DeviceIdType.MESH


def kernel(
    n, ns, li, cot, w, mid, gi, gs, gq,
    inc, lix, gis, ids, wv,
    perm_s, perm_r, right_s, left_s, cot_r, li_s, li_r, gi_s, gi_r, id_s, id_r, own_s,
):
    f = lax.axis_index("fsdp")
    s = lax.axis_index("section")
    behind = lax.rem(s + ns - 1, ns)
    ahead = lax.rem(s + 1, ns)
    tokens, share = lix.shape[1], lix.shape[2]
    columns = inc.shape[2]

    def share_of(ref, part, rows=slice(None)):
        return ref.at[rows, pl.ds(pl.multiple_of(part * share, share), share)]

    def li_copy(target, rows=slice(None)):
        return pltpu.make_async_remote_copy(
            src_ref=share_of(li, target, rows),
            dst_ref=lix.at[f, rows],
            send_sem=li_s.at[target],
            recv_sem=li_r.at[f],
            device_id={"fsdp": target},
            device_id_type=MESH,
        )

    def cot_copy(block, target, sem):
        return pltpu.make_async_remote_copy(
            src_ref=inc.at[block],
            dst_ref=inc.at[block],
            send_sem=sem.at[block],
            recv_sem=cot_r.at[block],
            device_id={"fsdp": target},
            device_id_type=MESH,
        )

    def gi_copy(target):
        return pltpu.make_async_remote_copy(
            src_ref=gis.at[target],
            dst_ref=share_of(gi, f),
            send_sem=gi_s.at[target],
            recv_sem=gi_r.at[f],
            device_id={"fsdp": target},
            device_id_type=MESH,
        )

    def id_copy(target):
        return pltpu.make_async_remote_copy(
            src_ref=ids.at[f],
            dst_ref=ids.at[f],
            send_sem=id_s.at[target],
            recv_sem=id_r.at[f],
            device_id={"fsdp": target},
            device_id_type=MESH,
        )

    barrier = pltpu.get_barrier_semaphore()
    pl.semaphore_signal(barrier, inc=1, device_id={"section": ahead}, device_id_type=MESH)
    for step in range(1, n):
        pl.semaphore_signal(
            barrier, inc=1, device_id={"fsdp": lax.rem(f + step, n)}, device_id_type=MESH
        )
    pl.semaphore_wait(barrier, n)

    permute = pltpu.make_async_remote_copy(
        src_ref=cot,
        dst_ref=inc.at[f],
        send_sem=perm_s,
        recv_sem=perm_r,
        device_id={"section": behind},
        device_id_type=MESH,
    )
    permute.start()

    pieces = min(n, 4)
    rows = tokens // pieces

    def li_piece(piece):
        if piece >= pieces:
            return
        window = pl.ds(piece * rows, rows)

        @pl.when(f < n - 1)
        def _():
            li_copy(n - 1, window).start()

        @pl.when(f > 0)
        def _():
            li_copy(0, window).start()

    def forward(step):
        @pl.when((f - step >= 0) & (f < n - 1))
        def _():
            cot_copy(f - step, f + 1, right_s).start()

        @pl.when((f + step < n) & (f > 0))
        def _():
            cot_copy(f + step, f - 1, left_s).start()

    def arrived(step):
        @pl.when(f - step >= 0)
        def _():
            cot_copy(f - step, f, right_s).wait_recv()

        @pl.when(f + step < n)
        def _():
            cot_copy(f + step, f, left_s).wait_recv()

    li_piece(0)
    weights = pltpu.make_async_copy(w, wv, own_s.at[0])
    weights.start()
    own_li = pltpu.make_async_copy(share_of(li, f), lix.at[f], own_s.at[1])
    own_li.start()
    ids[f] = jnp.full(ids.shape[1:], mid[0, 0], jnp.int32)
    permute.wait_recv()
    forward(0)
    for step in range(1, n):
        id_copy(lax.rem(f + step, n)).start()
    li_piece(1)
    for step in range(1, n - 1):
        arrived(step)
        forward(step)
        li_piece(step + 1)
    for piece in range(n, pieces):
        li_piece(piece)
    for turn in range(1, n - 1):
        @pl.when(n - 1 - turn > f)
        def _():
            li_copy(n - 1 - turn).start()

        @pl.when(turn < f)
        def _():
            li_copy(turn).start()
    arrived(n - 1)

    weights.wait()

    def input_block(block, carry):
        gis[block] = lax.dot_general(
            inc[block], wv[...], (((1,), (1,)), ((), ())), preferred_element_type=jnp.float32
        ).astype(gis.dtype)
        return carry

    lax.fori_loop(0, n, input_block, 0)
    own_gi = pltpu.make_async_copy(gis.at[f], share_of(gi, f), own_s.at[2])
    own_gi.start()
    for turn in range(n - 1):
        @pl.when(n - 1 - turn > f)
        def _():
            gi_copy(n - 1 - turn).start()

        @pl.when(turn < f)
        def _():
            gi_copy(turn).start()

    own_li.wait()

    def others(action):
        def run(step, carry):
            action(lax.rem(f + step, n))
            return carry

        lax.fori_loop(1, n, run, 0)

    def li_wait(peer):
        pltpu.make_async_remote_copy(
            src_ref=share_of(li, peer),
            dst_ref=lix.at[peer],
            send_sem=li_s.at[peer],
            recv_sem=li_r.at[peer],
            device_id={"fsdp": peer},
            device_id_type=MESH,
        ).wait()
        pltpu.make_async_remote_copy(
            src_ref=ids.at[f],
            dst_ref=ids.at[peer],
            send_sem=id_s.at[peer],
            recv_sem=id_r.at[peer],
            device_id={"fsdp": peer},
            device_id_type=MESH,
        ).wait()

    others(li_wait)

    inverse = 1.0 / tokens
    tile = 128

    def weight_rows(index, carry):
        start = pl.multiple_of(index * tile, tile)
        micro = [jnp.zeros((tile, columns), jnp.float32) for _ in range(MICRO)]
        for block in range(n):
            product = lax.dot_general(
                lix[block, :, pl.ds(start, tile)],
                inc[block],
                (((0,), (0,)), ((), ())),
                preferred_element_type=jnp.float32,
            )
            product = (product * inverse).astype(jnp.bfloat16).astype(jnp.float32)
            owner = jnp.broadcast_to(ids[block][:1, :1], product.shape)
            for m in range(MICRO):
                micro[m] = micro[m] + jnp.where(owner == m, product, 0.0)
        total = micro[0]
        square = micro[0] * micro[0]
        for m in range(1, MICRO):
            total = total + micro[m]
            square = square + micro[m] * micro[m]
        gs[pl.ds(start, tile), :] = total
        gq[pl.ds(start, tile), :] = square
        return carry

    lax.fori_loop(0, share // tile, weight_rows, 0)

    own_gi.wait()
    permute.wait_send()
    for step in range(n - 1):
        @pl.when((f - step >= 0) & (f < n - 1))
        def _():
            cot_copy(f - step, f + 1, right_s).wait_send()

        @pl.when((f + step < n) & (f > 0))
        def _():
            cot_copy(f + step, f - 1, left_s).wait_send()

    def gi_wait(peer):
        pltpu.make_async_remote_copy(
            src_ref=gis.at[peer],
            dst_ref=share_of(gi, peer),
            send_sem=gi_s.at[peer],
            recv_sem=gi_r.at[peer],
            device_id={"fsdp": peer},
            device_id_type=MESH,
        ).wait()

    others(gi_wait)


def settle_kernel(cuts, *refs):
    count = len(refs) // 2
    sems = refs[-1]
    copies = []
    for index in range(count):
        source, target = refs[index], refs[count + index]
        rows = source.shape[0] // cuts
        for cut in range(cuts):
            window = pl.ds(cut * rows, rows)
            copies.append(
                pltpu.make_async_copy(source.at[window], target.at[window], sems.at[index, cut])
            )
    for copy in copies:
        copy.start()
    for copy in copies:
        copy.wait()


def settle(*arrays):
    cuts = 1
    return pl.pallas_call(
        functools.partial(settle_kernel, cuts),
        out_shape=tuple(jax.ShapeDtypeStruct(a.shape, a.dtype) for a in arrays),
        in_specs=[pl.BlockSpec(memory_space=pl.ANY)] * len(arrays),
        out_specs=tuple(pl.BlockSpec(memory_space=pltpu.HBM) for _ in arrays),
        scratch_shapes=[pltpu.SemaphoreType.DMA((len(arrays), cuts))],
        compiler_params=pltpu.CompilerParams(vmem_limit_bytes=4 * 2**20),
    )(*[pltpu.with_memory_space_constraint(a, pltpu.VMEM) for a in arrays])


def body(layer_input, next_cot, w_value, micro_ids):
    n = lax.axis_size("fsdp")
    ns = lax.axis_size("section")
    tokens, width = layer_input.shape[1:]
    share, columns = w_value.shape[1:]
    anywhere = pl.BlockSpec(memory_space=pltpu.HBM)
    dma = pltpu.SemaphoreType.DMA
    stay = functools.partial(pltpu.with_memory_space_constraint, memory_space=pltpu.HBM)
    arrays = pl.pallas_call(
        functools.partial(kernel, n, ns),
        out_shape=(
            jax.ShapeDtypeStruct((tokens, width), jnp.bfloat16),
            jax.ShapeDtypeStruct((share, columns), jnp.float32),
            jax.ShapeDtypeStruct((share, columns), jnp.float32),
        ),
        in_specs=[anywhere, anywhere, anywhere, pl.BlockSpec(memory_space=pltpu.SMEM)],
        out_specs=OUT_SPECS,
        scratch_shapes=[
            pltpu.VMEM((n, tokens, columns), jnp.bfloat16),
            pltpu.VMEM((n, tokens, share), jnp.bfloat16),
            pltpu.VMEM((n, tokens, share), jnp.bfloat16),
            pltpu.VMEM((n, 8, 128), jnp.int32),
            pltpu.VMEM((share, columns), jnp.bfloat16),
            dma, dma, dma((n,)), dma((n,)), dma((n,)), dma((n,)), dma((n,)),
            dma((n,)), dma((n,)), dma((n,)), dma((n,)), dma((3,)),
        ],
        compiler_params=pltpu.CompilerParams(
            collective_id=0, has_side_effects=True, vmem_limit_bytes=40 * 2**20
        ),
    )(stay(layer_input[0]), stay(next_cot[0]), stay(w_value[0]), micro_ids)
    grad_input, grad_sum, grad_square = settle(*arrays)
    return (grad_input[None], grad_sum[None], grad_square[None])


OUT_SPECS = (
    pl.BlockSpec(memory_space=pl.ANY),
    pl.BlockSpec(memory_space=pltpu.VMEM),
    pl.BlockSpec(memory_space=pltpu.VMEM),
)


def solution(mesh):
    spec = P("section", "fsdp", None)
    return jax.shard_map(
        body,
        mesh=mesh,
        in_specs=(spec, spec, spec, P("section", "fsdp")),
        out_specs=(spec, spec, spec),
        check_vma=False,
    )
```

```python
import functools

import jax
import jax.numpy as jnp
from jax import lax
from jax.experimental import pallas as pl
from jax.experimental.pallas import tpu as pltpu
from jax.sharding import PartitionSpec as P

MICRO = 2
MESH = pl.DeviceIdType.MESH


def kernel(
    n, ns, li, cot, w, mid, gi, gs, gq,
    inc, lix, gis, ids, wv,
    perm_s, perm_r, right_s, left_s, cot_r, li_s, li_r, gi_s, gi_r, id_s, id_r, own_s,
):
    f = lax.axis_index("fsdp")
    s = lax.axis_index("section")
    behind = lax.rem(s + ns - 1, ns)
    ahead = lax.rem(s + 1, ns)
    tokens, share = lix.shape[1], lix.shape[2]
    columns = inc.shape[2]

    def share_of(ref, part, rows=slice(None)):
        return ref.at[rows, pl.ds(pl.multiple_of(part * share, share), share)]

    def li_copy(target, rows=slice(None)):
        return pltpu.make_async_remote_copy(
            src_ref=share_of(li, target, rows),
            dst_ref=lix.at[f, rows],
            send_sem=li_s.at[target],
            recv_sem=li_r.at[f],
            device_id={"fsdp": target},
            device_id_type=MESH,
        )

    def cot_copy(block, target, sem):
        return pltpu.make_async_remote_copy(
            src_ref=inc.at[block],
            dst_ref=inc.at[block],
            send_sem=sem.at[block],
            recv_sem=cot_r.at[block],
            device_id={"fsdp": target},
            device_id_type=MESH,
        )

    def gi_copy(target):
        return pltpu.make_async_remote_copy(
            src_ref=gis.at[target],
            dst_ref=share_of(gi, f),
            send_sem=gi_s.at[target],
            recv_sem=gi_r.at[f],
            device_id={"fsdp": target},
            device_id_type=MESH,
        )

    def id_copy(target):
        return pltpu.make_async_remote_copy(
            src_ref=ids.at[f],
            dst_ref=ids.at[f],
            send_sem=id_s.at[target],
            recv_sem=id_r.at[f],
            device_id={"fsdp": target},
            device_id_type=MESH,
        )

    barrier = pltpu.get_barrier_semaphore()
    pl.semaphore_signal(barrier, inc=1, device_id={"section": ahead}, device_id_type=MESH)
    for step in range(1, n):
        pl.semaphore_signal(
            barrier, inc=1, device_id={"fsdp": lax.rem(f + step, n)}, device_id_type=MESH
        )
    pl.semaphore_wait(barrier, n)

    permute = pltpu.make_async_remote_copy(
        src_ref=cot,
        dst_ref=inc.at[f],
        send_sem=perm_s,
        recv_sem=perm_r,
        device_id={"section": behind},
        device_id_type=MESH,
    )

    pieces = min(n, 4)
    rows = tokens // pieces

    def li_piece(piece):
        if piece >= pieces:
            return
        window = pl.ds(piece * rows, rows)

        @pl.when(f < n - 1)
        def _():
            li_copy(n - 1, window).start()

        @pl.when(f > 0)
        def _():
            li_copy(0, window).start()

    def forward(step):
        @pl.when((f - step >= 0) & (f < n - 1))
        def _():
            cot_copy(f - step, f + 1, right_s).start()

        @pl.when((f + step < n) & (f > 0))
        def _():
            cot_copy(f + step, f - 1, left_s).start()

    def arrived(step):
        @pl.when(f - step >= 0)
        def _():
            cot_copy(f - step, f, right_s).wait_recv()

        @pl.when(f + step < n)
        def _():
            cot_copy(f + step, f, left_s).wait_recv()

    li_piece(0)
    permute.start()
    weights = pltpu.make_async_copy(w, wv, own_s.at[0])
    weights.start()
    own_li = pltpu.make_async_copy(share_of(li, f), lix.at[f], own_s.at[1])
    own_li.start()
    ids[f] = jnp.full(ids.shape[1:], mid[0, 0], jnp.int32)
    permute.wait_recv()
    forward(0)
    for step in range(1, n):
        id_copy(lax.rem(f + step, n)).start()
    li_piece(1)
    for step in range(1, n - 1):
        arrived(step)
        forward(step)
        li_piece(step + 1)
    for piece in range(n, pieces):
        li_piece(piece)
    for turn in range(1, n - 1):
        @pl.when(n - 1 - turn > f)
        def _():
            li_copy(n - 1 - turn).start()

        @pl.when(turn < f)
        def _():
            li_copy(turn).start()
    arrived(n - 1)

    weights.wait()

    def input_block(block, carry):
        gis[block] = lax.dot_general(
            inc[block], wv[...], (((1,), (1,)), ((), ())), preferred_element_type=jnp.float32
        ).astype(gis.dtype)
        return carry

    lax.fori_loop(0, n, input_block, 0)
    own_gi = pltpu.make_async_copy(gis.at[f], share_of(gi, f), own_s.at[2])
    own_gi.start()
    for turn in range(n - 1):
        @pl.when(n - 1 - turn > f)
        def _():
            gi_copy(n - 1 - turn).start()

        @pl.when(turn < f)
        def _():
            gi_copy(turn).start()

    own_li.wait()

    def others(action):
        def run(step, carry):
            action(lax.rem(f + step, n))
            return carry

        lax.fori_loop(1, n, run, 0)

    def li_wait(peer):
        pltpu.make_async_remote_copy(
            src_ref=share_of(li, peer),
            dst_ref=lix.at[peer],
            send_sem=li_s.at[peer],
            recv_sem=li_r.at[peer],
            device_id={"fsdp": peer},
            device_id_type=MESH,
        ).wait()
        pltpu.make_async_remote_copy(
            src_ref=ids.at[f],
            dst_ref=ids.at[peer],
            send_sem=id_s.at[peer],
            recv_sem=id_r.at[peer],
            device_id={"fsdp": peer},
            device_id_type=MESH,
        ).wait()

    others(li_wait)

    inverse = 1.0 / tokens
    tile = 128

    def weight_rows(index, carry):
        start = pl.multiple_of(index * tile, tile)
        micro = [jnp.zeros((tile, columns), jnp.float32) for _ in range(MICRO)]
        for block in range(n):
            product = lax.dot_general(
                lix[block, :, pl.ds(start, tile)],
                inc[block],
                (((0,), (0,)), ((), ())),
                preferred_element_type=jnp.float32,
            )
            product = (product * inverse).astype(jnp.bfloat16).astype(jnp.float32)
            owner = jnp.broadcast_to(ids[block][:1, :1], product.shape)
            for m in range(MICRO):
                micro[m] = micro[m] + jnp.where(owner == m, product, 0.0)
        total = micro[0]
        square = micro[0] * micro[0]
        for m in range(1, MICRO):
            total = total + micro[m]
            square = square + micro[m] * micro[m]
        gs[pl.ds(start, tile), :] = total
        gq[pl.ds(start, tile), :] = square
        return carry

    lax.fori_loop(0, share // tile, weight_rows, 0)

    own_gi.wait()
    permute.wait_send()
    for step in range(n - 1):
        @pl.when((f - step >= 0) & (f < n - 1))
        def _():
            cot_copy(f - step, f + 1, right_s).wait_send()

        @pl.when((f + step < n) & (f > 0))
        def _():
            cot_copy(f + step, f - 1, left_s).wait_send()

    def gi_wait(peer):
        pltpu.make_async_remote_copy(
            src_ref=gis.at[peer],
            dst_ref=share_of(gi, peer),
            send_sem=gi_s.at[peer],
            recv_sem=gi_r.at[peer],
            device_id={"fsdp": peer},
            device_id_type=MESH,
        ).wait()

    others(gi_wait)


def settle_kernel(cuts, *refs):
    count = len(refs) // 2
    sems = refs[-1]
    copies = []
    for index in range(count):
        source, target = refs[index], refs[count + index]
        rows = source.shape[0] // cuts
        for cut in range(cuts):
            window = pl.ds(cut * rows, rows)
            copies.append(
                pltpu.make_async_copy(source.at[window], target.at[window], sems.at[index, cut])
            )
    for copy in copies:
        copy.start()
    for copy in copies:
        copy.wait()


def settle(*arrays):
    cuts = 1
    return pl.pallas_call(
        functools.partial(settle_kernel, cuts),
        out_shape=tuple(jax.ShapeDtypeStruct(a.shape, a.dtype) for a in arrays),
        in_specs=[pl.BlockSpec(memory_space=pl.ANY)] * len(arrays),
        out_specs=tuple(pl.BlockSpec(memory_space=pltpu.HBM) for _ in arrays),
        scratch_shapes=[pltpu.SemaphoreType.DMA((len(arrays), cuts))],
        compiler_params=pltpu.CompilerParams(vmem_limit_bytes=4 * 2**20),
    )(*[pltpu.with_memory_space_constraint(a, pltpu.VMEM) for a in arrays])


def body(layer_input, next_cot, w_value, micro_ids):
    n = lax.axis_size("fsdp")
    ns = lax.axis_size("section")
    tokens, width = layer_input.shape[1:]
    share, columns = w_value.shape[1:]
    anywhere = pl.BlockSpec(memory_space=pltpu.HBM)
    dma = pltpu.SemaphoreType.DMA
    stay = functools.partial(pltpu.with_memory_space_constraint, memory_space=pltpu.HBM)
    arrays = pl.pallas_call(
        functools.partial(kernel, n, ns),
        out_shape=(
            jax.ShapeDtypeStruct((tokens, width), jnp.bfloat16),
            jax.ShapeDtypeStruct((share, columns), jnp.float32),
            jax.ShapeDtypeStruct((share, columns), jnp.float32),
        ),
        in_specs=[anywhere, anywhere, anywhere, pl.BlockSpec(memory_space=pltpu.SMEM)],
        out_specs=OUT_SPECS,
        scratch_shapes=[
            pltpu.VMEM((n, tokens, columns), jnp.bfloat16),
            pltpu.VMEM((n, tokens, share), jnp.bfloat16),
            pltpu.VMEM((n, tokens, share), jnp.bfloat16),
            pltpu.VMEM((n, 8, 128), jnp.int32),
            pltpu.VMEM((share, columns), jnp.bfloat16),
            dma, dma, dma((n,)), dma((n,)), dma((n,)), dma((n,)), dma((n,)),
            dma((n,)), dma((n,)), dma((n,)), dma((n,)), dma((3,)),
        ],
        compiler_params=pltpu.CompilerParams(
            collective_id=0, has_side_effects=True, vmem_limit_bytes=40 * 2**20
        ),
    )(stay(layer_input[0]), stay(next_cot[0]), stay(w_value[0]), micro_ids)
    grad_input, grad_sum, grad_square = settle(*arrays)
    return (grad_input[None], grad_sum[None], grad_square[None])


OUT_SPECS = (
    pl.BlockSpec(memory_space=pl.ANY),
    pl.BlockSpec(memory_space=pltpu.VMEM),
    pl.BlockSpec(memory_space=pltpu.VMEM),
)


def solution(mesh):
    spec = P("section", "fsdp", None)
    return jax.shard_map(
        body,
        mesh=mesh,
        in_specs=(spec, spec, spec, P("section", "fsdp")),
        out_specs=(spec, spec, spec),
        check_vma=False,
    )
```
